32 devices in a mesh: dp: 8 (over y, x, core), mp: 4 (over z).
Axes of the slice: x: 2, y: 2, z: 4, core: 2. Of those that a mesh axis runs over, the one named last changes fastest.
Arguments:
- images: bfloat16 [16, 577, 1024], P('dp'), may hold values from -6 to 6
- w_qkv: bfloat16 [1024, 3, 1024], P(None, None, 'mp'), may hold values from -0.1875 to 0.1875
- qv_bias: float32 [2, 1024], P(None, 'mp'), may hold values from -2 to 2
- w_out: bfloat16 [1024, 1024], P('mp'), may hold values from -1 to 1
- b_out: float32 [1024], replicated, may hold values from -2 to 2
- w_fc1: bfloat16 [1024, 4096], P(None, 'mp'), may hold values from -0.1875 to 0.1875
- b_fc1: float32 [4096], P('mp'), may hold values from -2 to 2
- w_fc2: bfloat16 [4096, 1024], P('mp'), may hold values from -0.09375 to 0.09375
- b_fc2: float32 [1024], replicated, may hold values from -2 to 2
- ln_gain: float32 [2, 1024], replicated, may hold values from 0.5 to 1.5
- ln_bias: float32 [2, 1024], replicated, may hold values from -2 to 2
- cotangent: bfloat16 [16, 577, 1024], P('dp'), may hold values from -6 to 6
Outputs:
- block_out: bfloat16 [16, 577, 1024], P('dp')
- grad_images: bfloat16 [16, 577, 1024], P('dp')
- grad_w_qkv: float32 [1024, 3, 1024], P(None, None, 'mp')
- grad_qv_bias: float32 [2, 1024], P(None, 'mp')
- grad_w_out: float32 [1024, 1024], P('mp')
- grad_b_out: float32 [1024], replicated
- grad_w_fc1: float32 [1024, 4096], P(None, 'mp')
- grad_b_fc1: float32 [4096], P('mp')
- grad_w_fc2: float32 [4096, 1024], P('mp')
- grad_b_fc2: float32 [1024], replicated
- grad_ln_gain: float32 [2, 1024], replicated
- grad_ln_bias: float32 [2, 1024], replicated
The draws below stay inside these ranges and needn't reach their ends.
All inputs are finite; a program needn't handle non-finite values.
Results may differ from the reference program's by a relative error of at most 0.017.
Values may be sent and summed in bfloat16 or wider, within the bound.
No kernel may reach another device: no remote copies, remote signals or barrier semaphores. Data moves between devices by JAX's collectives and lax.ppermute only.
A program may use at most 192 MiB of HBM per device.

```python
from functools import partial
import jax
import jax.numpy as jnp
from jax import lax

D = 1024
HEADS = 16
HEAD_DIM = 64
FF = 4096
SEQ = 577
IMG_SHARD = 2
IMAGES = 16


def block_levels(own_key, extent, split, smallest, top_value):
    level, own = 1.0, jax.random.fold_in(own_key, 6)
    for dim, blocks in split:
        steps = jnp.exp(jax.random.uniform(jax.random.fold_in(own, dim), (blocks,), jnp.float32, smallest / len(split), top_value / len(split)))
        level = level * jnp.repeat(steps, extent[dim] // blocks).reshape([-1 if axis == dim else 1 for axis in range(len(extent))])
    return level


def bell_draw(rng, dims, spread, bound, split=(), kind=jnp.bfloat16):
    result = spread * jax.random.normal(rng, dims, jnp.float32)
    if split:
        result = result * block_levels(rng, dims, split, -0.22, 0.18)
    return jnp.clip(result, -bound, bound).astype(kind)


def setup_inputs(seed: int = 0) -> dict:
    streams_of = jax.random.split(jax.random.key(seed), 13)
    return {
        "images": bell_draw(streams_of[0], (IMAGES, SEQ, D), 1.0, 6.0, ((0, 8),)),
        "w_qkv": bell_draw(streams_of[1], (D, 3, D), D ** -0.5, 0.1875, ((2, 4),)),
        "qv_bias": bell_draw(streams_of[2], (2, D), 0.3, 2.0, ((1, 4),), jnp.float32),
        "w_out": bell_draw(streams_of[3], (D, D), (D // 32) ** -0.5, 1.0, ((0, 4),)),
        "b_out": bell_draw(streams_of[4], (D,), 0.3, 2.0, (), jnp.float32),
        "w_fc1": bell_draw(streams_of[5], (D, FF), D ** -0.5, 0.1875, ((1, 4),)),
        "b_fc1": bell_draw(streams_of[6], (FF,), 0.3, 2.0, ((0, 4),), jnp.float32),
        "w_fc2": bell_draw(streams_of[7], (FF, D), FF ** -0.5, 0.09375, ((0, 4),)),
        "b_fc2": bell_draw(streams_of[8], (D,), 0.3, 2.0, (), jnp.float32),
        "ln_gain": jnp.clip(1.0 + 0.1 * jax.random.normal(streams_of[9], (2, D), jnp.float32), 0.5, 1.5),
        "ln_bias": bell_draw(streams_of[10], (2, D), 0.3, 2.0, (), jnp.float32),
        "cotangent": bell_draw(streams_of[11], (IMAGES, SEQ, D), 1.0, 6.0, ((0, 8),)),
    }


@jax.custom_vjp
def low(v):
    return lax.optimization_barrier(v.astype(jnp.bfloat16)).astype(jnp.float32)

@jax.custom_vjp
def low_back(v):
    return v

def low_keep(v):
    return (low(v), None)

def low_pass(kept, grad):
    return (grad,)

def back_keep(v):
    return (v, None)

def back_low(kept, grad):
    return (low(grad),)
low.defvjp(low_keep, low_pass)
low_back.defvjp(back_keep, back_low)
epsilon = 1e-06
highest = lax.Precision.HIGHEST

def layer_norm(rows, gain, shift):
    mean = lax.optimization_barrier(jnp.mean(rows, axis=-1, keepdims=True))
    centred = rows - mean
    inverse = lax.rsqrt(lax.optimization_barrier(jnp.mean(centred * centred, axis=-1, keepdims=True)) + epsilon)
    return centred * inverse * gain + shift

def block(params, group):
    w_qkv, qv_bias, w_out, b_out, w_fc1, b_fc1, w_fc2, b_fc2, ln_gain, ln_bias = params
    count = group.shape[0]
    first = low(layer_norm(group, ln_gain[0], ln_bias[0]))
    proj = jnp.einsum('isd,dje->isje', first, w_qkv, precision=highest)
    query = low(low_back(proj[:, :, 0] + qv_bias[0]))
    key_rows = low(low_back(proj[:, :, 1]))
    value_rows = low(low_back(proj[:, :, 2] + qv_bias[1]))
    shape = (count, SEQ, HEADS, HEAD_DIM)
    query = query.reshape(shape)
    key_rows = key_rows.reshape(shape)
    value_rows = value_rows.reshape(shape)
    scores = low_back(jnp.einsum('iqhe,ikhe->ihqk', query, key_rows, precision=highest) * HEAD_DIM ** (-0.5))
    probs = low(jax.nn.softmax(scores, axis=-1))
    mixed = low(low_back(jnp.einsum('ihqk,ikhe->iqhe', probs, value_rows, precision=highest)))
    mixed = mixed.reshape(count, SEQ, D)
    attn = low_back(jnp.einsum('isd,de->ise', mixed, w_out, precision=highest))
    resid = group + attn + b_out
    second = low(layer_norm(resid, ln_gain[1], ln_bias[1]))
    hidden = low_back(jnp.einsum('isd,df->isf', second, w_fc1, precision=highest) + b_fc1)
    active = low(jax.nn.gelu(hidden, approximate=False))
    mlp = low_back(jnp.einsum('isf,fd->isd', active, w_fc2, precision=highest))
    return resid + mlp + b_fc2

def forward(inputs, params):
    grouped = inputs.reshape(IMAGES // IMG_SHARD, IMG_SHARD, SEQ, D)
    step_fn = jax.checkpoint(partial(block, params))

    def scan_step(carry, group):
        return (carry, step_fn(group))
    _, outputs = lax.scan(scan_step, jnp.zeros((), jnp.float32), grouped)
    return outputs.reshape(IMAGES, SEQ, D)

def reference(images, w_qkv, qv_bias, w_out, b_out, w_fc1, b_fc1, w_fc2, b_fc2, ln_gain, ln_bias, cotangent):
    params = (w_qkv.astype(jnp.float32), qv_bias.astype(jnp.float32), w_out.astype(jnp.float32), b_out.astype(jnp.float32), w_fc1.astype(jnp.float32), b_fc1.astype(jnp.float32), w_fc2.astype(jnp.float32), b_fc2.astype(jnp.float32), ln_gain.astype(jnp.float32), ln_bias.astype(jnp.float32))
    inputs = images.astype(jnp.float32)
    outputs, pullback = jax.vjp(forward, inputs, params)
    grad_inputs, grads = pullback(cotangent.astype(jnp.float32))
    return (outputs.astype(jnp.bfloat16), grad_inputs.astype(jnp.bfloat16), grads[0], grads[1], grads[2], grads[3], grads[4], grads[5], grads[6], grads[7], grads[8], grads[9])
```

```python
import itertools
from functools import partial

import jax
import jax.numpy as jnp
from jax import lax
from jax.experimental import pallas as pl
from jax.experimental.pallas import tpu as pltpu
from jax.sharding import Mesh
from jax.sharding import PartitionSpec as P

HEAD_DIM = 64
EPSILON = 1e-06
AXES = ("y", "x", "core", "hf", "pz")


def low(values):
    return values.astype(jnp.bfloat16)


def wide(values):
    return values.astype(jnp.float32)


def unit_rows(rows):
    centred = rows - jnp.mean(rows, axis=-1, keepdims=True)
    inverse = lax.rsqrt(jnp.mean(centred * centred, axis=-1, keepdims=True) + EPSILON)
    return centred * inverse, inverse


def norm_back(grad, unit, inverse, gain):
    scaled = grad * gain
    inner = (
        scaled
        - jnp.mean(scaled, axis=-1, keepdims=True)
        - unit * jnp.mean(scaled * unit, axis=-1, keepdims=True)
    )
    return inner * inverse, jnp.sum(grad * unit, axis=0), jnp.sum(grad, axis=0)


def dot(left, right, dims):
    return lax.dot_general(left, right, (dims, ((), ())), preferred_element_type=jnp.float32)


PLAIN, ROWS, TRANSPOSED = ((1,), (0,)), ((0,), (0,)), ((1,), (1,))


def prepare_kernel(seq, part_rows, parts, with_norm, place, own, other, *refs):
    if with_norm:
        gain, shift, out, held = refs
    else:
        (out,) = refs
    part = lax.rem(place[1] + 1 + pl.program_id(1), parts)
    rows = wide(jnp.where(place[2] == 1, own[0], other[0]))
    index = part * part_rows + lax.broadcasted_iota(jnp.int32, rows.shape, 0)
    rows = jnp.where(index < seq, rows, 0.0)
    if with_norm:
        held[...] = low(rows)
        unit, _ = unit_rows(rows)
        out[...] = low(unit * gain[...] + shift[...])
    else:
        out[...] = low(rows)


def prepare(place, own, other, parts, part_rows, norm=None):
    shard, seq, width = own.shape
    total = shard * parts * part_rows

    def pick(wanted):
        def index(i, j, place):
            live = place[2] == wanted
            image = lax.rem(place[0] + 1 + i, 2)
            part = lax.rem(place[1] + 1 + j, parts)
            return (jnp.where(live, image, 0), jnp.where(live, part, 0), 0)

        return index

    block = (1, part_rows, width)
    in_specs = [pl.BlockSpec(block, pick(1)), pl.BlockSpec(block, pick(0))]
    out_specs = [pl.BlockSpec((part_rows, width), lambda i, j, place: (i * parts + j, 0))]
    out_shape = [jax.ShapeDtypeStruct((total, width), jnp.bfloat16)]
    args = [place, own, other]
    if norm is not None:
        in_specs += [pl.BlockSpec((1, width), lambda i, j, place: (0, 0))] * 2
        out_specs.append(pl.BlockSpec((part_rows, width), lambda i, j, place: (0, 0)))
        out_shape.append(jax.ShapeDtypeStruct((part_rows, width), jnp.bfloat16))
        args += [norm[0], norm[1]]
    return pl.pallas_call(
        partial(prepare_kernel, seq, part_rows, parts, norm is not None),
        grid_spec=pltpu.PrefetchScalarGridSpec(
            num_scalar_prefetch=1, grid=(shard, parts), in_specs=in_specs, out_specs=out_specs
        ),
        out_shape=out_shape,
        cost_estimate=pl.CostEstimate(
            flops=total * width * 8, bytes_accessed=total * width * 4, transcendentals=0
        ),
        name="prepare",
    )(*args)


def probs_of(query, key_rows, mask):
    scores = dot(query, key_rows, TRANSPOSED) * (HEAD_DIM**-0.5) + mask
    grown = jnp.exp(scores - jnp.max(scores, axis=-1, keepdims=True))
    return grown * (1.0 / jnp.sum(grown, axis=-1, keepdims=True))


def attend_kernel(query, key_rows, value_rows, mask, mixed):
    for head in range(mixed.shape[1] // HEAD_DIM):
        at = slice(head * HEAD_DIM, (head + 1) * HEAD_DIM)
        probs = probs_of(query[:, at], key_rows[:, at], mask[...])
        mixed[:, at] = low(dot(low(probs), value_rows[:, at], PLAIN))


def attend_back_kernel(query, key_rows, value_rows, grad_mixed, mask, grad_proj):
    local = grad_mixed.shape[1]
    for head in range(local // HEAD_DIM):
        at = slice(head * HEAD_DIM, (head + 1) * HEAD_DIM)
        q, k, v, g = query[:, at], key_rows[:, at], value_rows[:, at], grad_mixed[:, at]
        probs = probs_of(q, k, mask[...])
        grad_probs = dot(g, v, TRANSPOSED)
        grad_scores = probs * (grad_probs - jnp.sum(grad_probs * probs, axis=-1, keepdims=True))
        grad_scores = low(grad_scores)
        start = head * HEAD_DIM
        grad_proj[:, start : start + HEAD_DIM] = low(dot(grad_scores, k, PLAIN) * (HEAD_DIM**-0.5))
        start += local
        grad_proj[:, start : start + HEAD_DIM] = low(dot(grad_scores, q, ROWS) * (HEAD_DIM**-0.5))
        start += local
        grad_proj[:, start : start + HEAD_DIM] = low(dot(low(probs), g, ROWS))


def attention(proj, mask, padded, grad_mixed=None):
    total, local = proj.shape[0], proj.shape[1] // 3
    images = total // padded
    square = images * (local // HEAD_DIM) * padded * padded
    in_specs = [pl.BlockSpec((padded, local), partial(lambda n, i: (i, n), n)) for n in range(3)]
    args = [proj, proj, proj]
    kernel, width, dots = attend_kernel, local, 2
    if grad_mixed is not None:
        in_specs.append(pl.BlockSpec((padded, local), lambda i: (i, 0)))
        args.append(grad_mixed)
        kernel, width, dots = attend_back_kernel, 3 * local, 5
    in_specs.append(pl.BlockSpec((1, padded), lambda i: (0, 0)))
    return pl.pallas_call(
        kernel,
        grid=(images,),
        in_specs=in_specs,
        out_specs=pl.BlockSpec((padded, width), lambda i: (i, 0)),
        out_shape=jax.ShapeDtypeStruct((total, width), jnp.bfloat16),
        cost_estimate=pl.CostEstimate(
            flops=dots * 2 * square * 256, bytes_accessed=total * local * 8, transcendentals=square
        ),
        name="attend" if grad_mixed is None else "attend_back",
    )(*args, mask)


def body(
    sizes,
    images,
    w_qkv,
    qv_bias,
    w_out,
    b_out,
    w_fc1,
    b_fc1,
    w_fc2,
    b_fc2,
    ln_gain,
    ln_bias,
    cotangent,
):
    shard, seq, width = images.shape
    across, parts = sizes["x"], sizes["pz"]
    local = w_qkv.shape[2]
    part_rows = -(-seq // (16 * parts)) * 16
    padded = parts * part_rows
    at = {name: lax.axis_index(name) for name in AXES}
    home = at["core"] == at["hf"]

    def move(values, axes, to):
        def number(place):
            index = 0
            for axis in axes:
                index = index * sizes[axis] + place[axis]
            return index

        pairs = []
        for place in itertools.product(*(range(sizes[axis]) for axis in axes)):
            place = dict(zip(axes, place))
            target = to(dict(place))
            if target is not None:
                pairs.append((number(place), number(target)))
        return lax.ppermute(values, axes, pairs)

    def flip(values, axis, at_home=None):
        used = {axis} if at_home is None else {axis, "core", "hf"}
        axes = tuple(name for name in AXES if name in used)

        def to(place):
            if at_home is not None and (place["core"] == place["hf"]) != at_home:
                return None
            place[axis] = 1 - place[axis]
            return place

        return move(values, axes, to)

    def shift(values, axis, by):
        return move(values, (axis,), lambda place: {axis: (place[axis] + by) % sizes[axis]})

    def plane_gather(piece, at_home):
        if across != 2:
            return lax.all_gather(piece, ("y", "x"), axis=0, tiled=True)
        half = piece.shape[0] // 2
        from_y = flip(piece, "y", at_home)
        from_x = flip(piece, "x", at_home)
        across_both = jnp.concatenate(
            [flip(from_y[:half], "x", at_home), flip(from_x[half:], "y", at_home)]
        )
        left = at["x"] == 0
        mine = [jnp.where(left, piece, from_x), jnp.where(left, from_x, piece)]
        theirs = [jnp.where(left, from_y, across_both), jnp.where(left, across_both, from_y)]
        return jnp.where(
            at["y"] == 0, jnp.concatenate(mine + theirs), jnp.concatenate(theirs + mine)
        )

    def fetch(own):
        quarter = own.shape[0] // (2 * across)
        index = at["y"] * across + at["x"]
        piece = lax.dynamic_slice_in_dim(own, index * quarter, quarter, 0)
        moved = flip(piece, "hf", True)
        if across != 2:
            moved = jnp.where(home, piece, moved)
        return jnp.where(home, own, plane_gather(moved, False))

    def plane_reduce(grads):
        if across != 2:
            return wide(lax.psum_scatter(grads, ("y", "x"), scatter_dimension=0, tiled=True))
        quarter = grads.shape[0] // 4
        half = quarter // 2

        def piece(y, x):
            return lax.dynamic_slice_in_dim(grads, (y * 2 + x) * quarter, quarter, 0)

        y, x = at["y"], at["x"]
        far = piece(1 - y, 1 - x)
        to_y, to_x = piece(1 - y, x), piece(y, 1 - x)
        first = low(wide(to_y[:half]) + wide(flip(far[:half], "x")))
        second = low(wide(to_x[half:]) + wide(flip(far[half:], "y")))
        from_y = flip(jnp.concatenate([first, to_y[half:]]), "y")
        from_x = flip(jnp.concatenate([to_x[:half], second]), "x")
        return wide(piece(y, x)) + wide(from_y) + wide(from_x)

    def reduce_weight(grads):
        piece = plane_reduce(grads)
        piece = low(piece + wide(flip(low(piece), "hf", False)))
        gathered = plane_gather(piece, True)
        return wide(jnp.where(home, gathered, flip(gathered, "core", True)))

    def group_reduce(partial_sums):
        kept = partial_sums[padded:] + wide(flip(low(partial_sums[:padded]), "core"))
        mine = kept[-part_rows:]
        for step in range(1, parts):
            piece = low(kept[(step - 1) * part_rows : step * part_rows])
            mine = mine + wide(shift(piece, "pz", step))
        return mine

    def group_gather(mine):
        pieces = [shift(mine, "pz", step) for step in range(parts - 1, 0, -1)]
        image = jnp.concatenate(pieces + [mine])
        return jnp.concatenate([flip(image, "core"), image])

    def spread(mine):
        both = jnp.stack([flip(mine, "core", False), mine])
        if parts == 2:

            def chain(values, out, edge=False):
                def to(place):
                    z = place["hf"] * 2 + place["pz"]
                    step = 1 if place["core"] == 0 else -1
                    first = 0 if place["core"] == 0 else 3
                    if (z - first) * step not in out:
                        return None
                    z += -step if edge else step
                    place["hf"], place["pz"] = z // 2, z % 2
                    return place

                return move(values, ("core", "hf", "pz"), to)

            one = chain(both, (0, 1))
            back = chain(both, (1,), True)
            two = chain(one, (1, 2))
            three = chain(two, (2,))
            z = at["hf"] * 2 + at["pz"]
            far = jnp.where(at["core"] == 0, z, 3 - z)
            outer = jnp.where(
                far == 0, both, jnp.where(far == 1, one, jnp.where(far == 2, two, three))
            )
            inner = jnp.where(
                far == 0, back, jnp.where(far == 1, both, jnp.where(far == 2, one, two))
            )
            order = at["core"] == 0
            pieces = [jnp.where(order, outer, inner), jnp.where(order, inner, outer)]
        else:
            rows = [both] + [shift(both, "pz", step) for step in range(1, parts)]
            rows = [jnp.where(home, row, flip(row, "hf", True)) for row in rows]
            stacked = jnp.stack(rows)
            pieces = [
                lax.dynamic_index_in_dim(
                    stacked, lax.rem(at["pz"] - part + parts, parts), keepdims=False
                )
                for part in range(parts)
            ]
        whole = jnp.concatenate(pieces, axis=1)[:, :seq]
        return jnp.where(at["core"] == 0, whole[::-1], whole)

    def total(values, axes):
        for axis in axes:
            span = 1
            while span < sizes[axis]:
                values = values + move(values, (axis,), lambda place: {axis: place[axis] ^ span})
                span *= 2
        return values

    place = jnp.stack([at["core"], at["pz"], home.astype(jnp.int32)]).astype(jnp.int32)
    other_images = flip(images, "core", True)
    qkv = fetch(w_qkv.reshape(width, 3 * local))
    out_weight = fetch(w_out)
    fc1 = fetch(w_fc1)
    fc2 = fetch(w_fc2)
    other_cotangent = flip(cotangent, "core", True)
    offsets = jnp.concatenate([qv_bias, b_fc1.reshape(-1, local)])
    offsets = jnp.where(home, offsets, flip(offsets, "hf", True))
    qkv_bias = jnp.concatenate([offsets[0], jnp.zeros_like(offsets[0]), offsets[1]])
    fc1_bias = offsets[2:].reshape(-1)

    first_low, held = prepare(
        place, images, other_images, parts, part_rows, (ln_gain[:1], ln_bias[:1])
    )
    (grad_out,) = prepare(place, cotangent, other_cotangent, parts, part_rows)
    token = jnp.arange(padded, dtype=jnp.int32)[None]
    token_part = lax.rem(at["pz"] + 1 + token // part_rows, parts)
    token = token_part * part_rows + token % part_rows
    mask = jnp.where(token < seq, 0.0, -1e30).astype(jnp.float32)

    proj = low(dot(first_low, qkv, PLAIN) + qkv_bias)
    mixed = attention(proj, mask, padded)
    attn = group_reduce(dot(mixed, out_weight, PLAIN))
    held = wide(held)
    resid = held + attn + b_out
    unit_two, inv_two = unit_rows(resid)
    second_low = group_gather(low(unit_two * ln_gain[1] + ln_bias[1]))
    hidden = dot(second_low, fc1, PLAIN) + fc1_bias
    half_erf = 0.5 * lax.erf(hidden * (0.5**0.5)) + 0.5
    active = low(hidden * half_erf)
    mlp = group_reduce(dot(active, fc2, PLAIN))
    block_out = spread(low(resid + mlp + b_fc2))

    slope = half_erf + hidden * jnp.exp(-0.5 * hidden * hidden) * (0.5 / jnp.pi) ** 0.5
    grad_hidden = low(dot(grad_out, fc2, TRANSPOSED) * slope)
    grad_second = group_reduce(dot(grad_hidden, fc1, TRANSPOSED))
    grad_norm_two, gain_two, shift_two = norm_back(grad_second, unit_two, inv_two, ln_gain[1])
    grad_out_mine = wide(grad_out[-part_rows:])
    grad_resid = grad_out_mine + grad_norm_two
    grad_attn = group_gather(low(grad_resid))
    grad_fc2 = reduce_weight(low(dot(active, grad_out, ROWS)))
    grad_fc1 = reduce_weight(low(dot(second_low, grad_hidden, ROWS)))
    grad_mixed = low(dot(grad_attn, out_weight, TRANSPOSED))
    grad_wout = reduce_weight(low(dot(mixed, grad_attn, ROWS)))
    grad_proj = attention(proj, mask, padded, grad_mixed)
    grad_first = group_reduce(dot(grad_proj, qkv, TRANSPOSED))
    grad_qkv = reduce_weight(low(dot(first_low, grad_proj, ROWS)))
    unit_one, inv_one = unit_rows(held)
    grad_norm_one, gain_one, shift_one = norm_back(grad_first, unit_one, inv_one, ln_gain[0])
    grad_images = spread(low(grad_resid + grad_norm_one))

    grad_b1 = jnp.sum(wide(grad_hidden), axis=0)
    grad_qv = jnp.sum(wide(grad_proj), axis=0)
    small_shard = jnp.concatenate([grad_b1, grad_qv])
    small_all = jnp.concatenate(
        [
            jnp.sum(grad_resid, axis=0),
            jnp.sum(grad_out_mine, axis=0),
            gain_one,
            gain_two,
            shift_one,
            shift_two,
        ]
    )
    cut = small_all.shape[0]
    vectors = total(jnp.concatenate([small_all, small_shard]), ("y", "x", "hf"))
    swapped = flip(vectors, "core")
    small_all = total(vectors[:cut] + swapped[:cut], ("pz",)).reshape(6, width)
    small_shard = jnp.where(home, vectors[cut:], swapped[cut:])
    hidden_units = grad_b1.shape[0]
    grad_b1, grad_qv = small_shard[:hidden_units], small_shard[hidden_units:].reshape(3, local)
    return (
        block_out,
        grad_images,
        grad_qkv.reshape(width, 3, local),
        jnp.stack([grad_qv[0], grad_qv[2]]),
        grad_wout,
        small_all[0],
        grad_fc1,
        grad_b1,
        grad_fc2,
        small_all[1],
        small_all[2:4],
        small_all[4:6],
    )


def solution(mesh):
    sizes = (2, mesh.shape["dp"] // 4, 2, 2, mesh.shape["mp"] // 2)
    split = Mesh(mesh.devices.reshape(sizes), AXES)
    dp, mp = ("y", "x", "core"), ("hf", "pz")
    rows, both = P(dp, None, None), P(None, mp)
    qkv, down, one = P(None, None, mp), P(mp, None), P(mp)
    return jax.shard_map(
        partial(body, dict(zip(AXES, sizes))),
        mesh=split,
        in_specs=(rows, qkv, both, down, P(), both, one, down, P(), P(), P(), rows),
        out_specs=(rows, rows, qkv, both, down, P(), both, one, down, P(), P(), P()),
        check_vma=False,
    )
```
